128 devices in a mesh: section: 4 (over z), seq: 32 (over y, x, core).
Axes of the slice: x: 4, y: 4, z: 4, core: 2. Of those that a mesh axis runs over, the one named last changes fastest.
Arguments:
- queries: bfloat16 [4, 4096, 8192], P('section', 'seq'), may hold values from -24 to 24
- keys: bfloat16 [4, 4096, 1024], P('section', 'seq'), may hold values from -24 to 24
- values: bfloat16 [4, 4096, 1024], P('section', 'seq'), may hold values from -6 to 6
- block_mask: int32 [4, 32, 32], P('section'), may hold values from 0 to 1, as said below
- block_live: int32 [4, 32], P('section'), may hold values from 1 to 128, as said below
Outputs:
- passed_context: bfloat16 [4, 4096, 8192], P('section', 'seq')
The draws below stay inside these ranges and needn't reach their ends.
Inputs may be any that keep to these rules, and one draw needn't show every extreme that they name: block_mask[m, i, j] is 1 exactly when block j is block i or one of its ancestors in micro-batch m's tree: the first 16 blocks form a chain, each later block hangs below the chain's last block or a later block of lower index. `block_live`: the first 16 blocks of every micro-batch are full, its last block holds one live token.
All inputs are finite; a program needn't handle non-finite values.
Results may differ from the reference program's by a relative error of at most 0.0049.
Values may be sent and summed in bfloat16 or wider, within the bound.
A program may use at most 128 MiB of HBM per device.

```python
import jax
import jax.numpy as jnp
from jax import lax

QUERY_HEADS = 64
KEY_VALUE_HEADS = 8
HEAD_SIZE = 128
BLK = 128
MICRO_BATCHES = 4
MICRO_SLOTS = 4096
NB = 32


def draw_queries(key, part):
    array_shape = (MICRO_BATCHES, MICRO_SLOTS, QUERY_HEADS * HEAD_SIZE)
    base = jnp.clip(jax.random.normal(jax.random.fold_in(key, 1), array_shape, jnp.float32), -6.0, 6.0)
    return base.astype(jnp.bfloat16)


def draw_keys(key, part):
    array_shape = (MICRO_BATCHES, MICRO_SLOTS, KEY_VALUE_HEADS * HEAD_SIZE)
    base = jnp.clip(jax.random.normal(jax.random.fold_in(key, 2), array_shape, jnp.float32), -6.0, 6.0)
    return base.astype(jnp.bfloat16)


def draw_block_mask(key, part):
    half = NB // 2
    index = jnp.arange(NB, dtype=jnp.int32)
    raw = jax.random.randint(jax.random.fold_in(key, 21), (MICRO_BATCHES, NB), 0, 1 << 20)
    spread = jnp.maximum(index - half + 1, 1)
    parent = jnp.where(index < half, index - 1, half - 1 + raw % spread[None, :])

    def step(block, ancestry):
        parent_now = parent[:, block]
        inherited = jnp.take_along_axis(ancestry, jnp.maximum(parent_now, 0)[:, None, None], axis=1)[:, 0, :]
        inherited = jnp.where((parent_now >= 0)[:, None], inherited, 0)
        own = (index == block).astype(jnp.int32)[None, :]
        return ancestry.at[:, block, :].set(jnp.maximum(inherited, own))
    return lax.fori_loop(0, NB, step, jnp.zeros((MICRO_BATCHES, NB, NB), jnp.int32))


def draw_block_live(key, part):
    index = jnp.arange(NB, dtype=jnp.int32)
    counts = jax.random.randint(jax.random.fold_in(key, 31), (MICRO_BATCHES, NB), 1, BLK + 1)
    counts = jnp.where(index[None, :] < NB // 2, BLK, counts)
    counts = jnp.where(index[None, :] == NB - 1, 1, counts)
    return counts.astype(jnp.int32)


def block_levels(rng, shape, cuts, low, high):
    def one(dim, blocks):
        steps = jax.random.uniform(jax.random.fold_in(jax.random.fold_in(rng, 6), dim), (blocks,), jnp.float32, low / len(cuts), high / len(cuts))
        return jnp.repeat(jnp.exp(steps), shape[dim] // blocks).reshape((-1,) + (1,) * (len(shape) - dim - 1))

    factor_of = one(*cuts[0])
    for cut in cuts[1:]:
        factor_of = factor_of * one(*cut)
    return factor_of


def normal_values(own_key, shape, scale, limit, split=(), held_as=jnp.bfloat16):
    entries = scale * jax.random.normal(own_key, shape, jnp.float32)
    if split:
        entries = entries * block_levels(own_key, shape, split, -0.22, 0.18)
    return jnp.clip(entries, -limit, limit).astype(held_as)


def setup_inputs(seed: int = 0) -> dict:
    streams_of = jax.random.split(jax.random.key(seed), 6)
    queries = draw_queries(jax.random.fold_in(streams_of[5], 71), 0)
    keys = draw_keys(jax.random.fold_in(streams_of[5], 71), 0)
    values = normal_values(streams_of[2], (MICRO_BATCHES, MICRO_SLOTS, KEY_VALUE_HEADS * HEAD_SIZE), 1.0, 6.0, ((0, 4), (1, 32)))
    block_mask = draw_block_mask(jax.random.fold_in(streams_of[5], 71), 0)
    block_live = draw_block_live(jax.random.fold_in(streams_of[5], 71), 0)
    return dict(queries=queries, keys=keys, values=values, block_mask=block_mask, block_live=block_live)


def attend(qrows, qpos, keys_h, values_h, block_mask, block_live):
    total = keys_h.shape[0]
    nblk = block_mask.shape[0]
    width = total // nblk
    kpos = jnp.arange(total, dtype=jnp.int32)
    kblock = kpos // width
    key_live = (kpos % width) < jnp.repeat(block_live, width)
    qblock = qpos // width
    pick = (qblock[:, None] == jnp.arange(nblk, dtype=jnp.int32)[None, :]).astype(jnp.float32)
    allowed = jnp.repeat(jnp.dot(pick, block_mask.astype(jnp.float32)) > 0.5, width, axis=1)
    allowed = allowed & key_live[None, :] & ((kblock[None, :] != qblock[:, None]) | (kpos[None, :] <= qpos[:, None]))
    q_live = (qpos % width).astype(jnp.float32) < jnp.dot(pick, block_live.astype(jnp.float32))
    scale = qrows.shape[-1] ** -0.5
    scores = jnp.einsum("rgd,kd->grk", qrows.astype(jnp.float32), keys_h.astype(jnp.float32)) * scale
    scores = jnp.where(allowed[None], scores, -1e30)
    top = jnp.max(scores, axis=-1, keepdims=True)
    expo = jnp.where(allowed[None], jnp.exp(scores - top), 0.0)
    weights = (expo / jnp.sum(expo, axis=-1, keepdims=True)).astype(jnp.bfloat16)
    context = jnp.einsum("grk,kd->rgd", weights.astype(jnp.float32), values_h.astype(jnp.float32))
    return jnp.where(q_live[:, None, None], context, 0.0).astype(jnp.bfloat16)


def reference(queries, keys, values, block_mask, block_live):
    query_group_size = QUERY_HEADS // KEY_VALUE_HEADS

    def micro(items):
        single_query, single_key, single_value, mask_one, live_one = items
        query_head_rows = single_query.reshape(MICRO_SLOTS, KEY_VALUE_HEADS, query_group_size, HEAD_SIZE).transpose(1, 0, 2, 3)
        key_head_rows = single_key.reshape(MICRO_SLOTS, KEY_VALUE_HEADS, HEAD_SIZE).transpose(1, 0, 2)
        value_head_rows = single_value.reshape(MICRO_SLOTS, KEY_VALUE_HEADS, HEAD_SIZE).transpose(1, 0, 2)

        def head(hitems):
            q_group, k_head, v_head = hitems
            q_blocks = q_group.reshape(NB, BLK, query_group_size, HEAD_SIZE)
            starts = jnp.arange(NB, dtype=jnp.int32) * BLK

            def block_fn(bitems):
                return attend(bitems[0], bitems[1] + jnp.arange(BLK, dtype=jnp.int32), k_head, v_head, mask_one, live_one)

            return lax.map(block_fn, (q_blocks, starts)).reshape(MICRO_SLOTS, query_group_size, HEAD_SIZE)

        out = lax.map(head, (query_head_rows, key_head_rows, value_head_rows))
        return out.transpose(1, 0, 2, 3).reshape(MICRO_SLOTS, QUERY_HEADS * HEAD_SIZE)

    results = lax.map(micro, (queries, keys, values, block_mask, block_live))
    return jnp.roll(results, 1, axis=0)
```

```python
import jax
import jax.numpy as jnp
from jax import lax
from jax.experimental import pallas as pl
from jax.experimental.pallas import tpu as pltpu
from jax.sharding import PartitionSpec as P

QUERY_HEADS = 64
KEY_VALUE_HEADS = 8
HEAD_SIZE = 128
BLK = 128
NB = 32
PHASES = 4
UNIT = 2
UNITS = 8 // UNIT
ROWS = 2 * BLK * UNIT
CH = 512
COEF = 1.4426950408889634 * HEAD_SIZE ** (-0.5)
NEG = -1e30


def col(start, size):
    return pl.ds(pl.multiple_of(start, 128), size)


def kernel(
    mask_ref, live_ref, q_hbm, k_hbm, v_hbm, out_hbm,
    kbuf, vbuf, qbuf, obuf, sbuf, bias, mbuf, mcbuf, lbuf, acc,
    r1, r2, r3, rq, ro, s1, s2, s3, sq, so,
):
    z = lax.axis_index("section")
    s = lax.axis_index("seq")
    core = lax.rem(s, 2)
    chip = s // 2
    x = lax.rem(chip, 4)
    y = chip // 4

    def at(xx, yy, kk):
        return {"seq": (lax.rem(yy, 4) * 4 + lax.rem(xx, 4)) * 2 + kk}

    def across(dz, kk):
        return {"section": lax.rem(z + dz, 4), "seq": chip * 2 + kk}

    other = {"seq": chip * 2 + 1 - core}

    def remote(src, dst, send, recv, dev):
        return pltpu.make_async_remote_copy(
            src_ref=src, dst_ref=dst, send_sem=send, recv_sem=recv,
            device_id=dev, device_id_type=pl.DeviceIdType.MESH,
        )

    barrier = pltpu.get_barrier_semaphore()
    partners = [other]
    for d in (1, 2, 3):
        for kk in (0, 1):
            partners.append(at(x + d, y, kk))
            partners.append(at(x, y + d, kk))
    for d in (1, 3):
        for kk in (0, 1):
            partners.append(across(d, kk))
    for dev in partners:
        pl.semaphore_signal(barrier, inc=1, device_id=dev, device_id_type=pl.DeviceIdType.MESH)
    pl.semaphore_wait(barrier, len(partners))

    pairs = ((k_hbm, kbuf), (v_hbm, vbuf))

    def stage1(p):
        for n, (src_hbm, buf) in enumerate(pairs):
            dst = buf.at[y, x, pl.ds(core * BLK, BLK), col(p * 128, 128)]
            for g in (0, 1):
                src = src_hbm.at[0, :, col((4 * g + p) * 128, 128)]
                @pl.when(core == g)
                def _():
                    pltpu.make_async_copy(src, dst, r1.at[p, n]).start()
                @pl.when(core != g)
                def _():
                    remote(src, dst, s1.at[n, 0], r1.at[p, n], other).start()
                for d in (1, 3, 2):
                    dev = at(x + d, y, 0) if g == 0 else at(x, y + d, 1)
                    remote(src, dst, s1.at[n, 3 * g + d], r1.at[p, n], dev).start()

    def queries(p):
        dst = qbuf.at[core, :, col(p * 1024, 1024)]
        pltpu.make_async_copy(q_hbm.at[0, :, col(core * 4096 + p * 1024, 1024)], dst, rq.at[p]).start()
        remote(q_hbm.at[0, :, col((1 - core) * 4096 + p * 1024, 1024)], dst, sq, rq.at[p], other).start()

    def wait_on(ref, sem):
        pltpu.make_async_copy(ref, ref, sem).wait()

    def stage2(p):
        for n, (_, buf) in enumerate(pairs):
            wait_on(buf.at[0, :, :, col(p * 128, 128)], r1.at[p, n])
        for n, (_, buf) in enumerate(pairs):
            for side, d in ((0, 1), (1, 3)):
                @pl.when(core == 0)
                def _():
                    slab = buf.at[y, :, :, col(p * 128, 128)]
                    remote(slab, slab, s2.at[n, side], r2.at[p, n, side], at(x, y + d, 0)).start()
                @pl.when(core == 1)
                def _():
                    slab = buf.at[:, x, :, col(p * 128, 128)]
                    remote(slab, slab, s2.at[n, side], r2.at[p, n, side], at(x + d, y, 1)).start()

    def stage3(p):
        for n, (_, buf) in enumerate(pairs):
            for side, d in ((0, 1), (1, 3)):
                wait_on(buf.at[0, :, :, col(p * 128, 128)], r2.at[p, n, side])
        for n, (_, buf) in enumerate(pairs):
            for side, d in ((0, 1), (1, 3)):
                @pl.when(core == 0)
                def _():
                    half = buf.at[lax.rem(y + 4 - d, 4), pl.ds(2 * side, 2), :, col(p * 128, 128)]
                    remote(half, half, s3.at[n, side], r3.at[p, n, side], at(x, y + d, 0)).start()
                @pl.when(core == 1)
                def _():
                    half = buf.at[pl.ds(2 * side, 2), lax.rem(x + 4 - d, 4), :, col(p * 128, 128)]
                    remote(half, half, s3.at[n, side], r3.at[p, n, side], at(x + d, y, 1)).start()

    def arrived(p):
        for n, (_, buf) in enumerate(pairs):
            for side in (0, 1):
                wait_on(buf.at[0, pl.ds(0, 2), :, col(p * 128, 128)], r3.at[p, n, side])
        wait_on(qbuf.at[:, :, col(p * 1024, 1024)], rq.at[p])

    stage1(0)
    queries(0)

    rows = lax.broadcasted_iota(jnp.int32, (BLK, BLK), 0)
    cols = lax.broadcasted_iota(jnp.int32, (BLK, BLK), 1)

    def fill(b, carry):
        for i in (0, 1):
            row = 2 * chip + i
            upto = live_ref[0, b] * mask_ref[0, row, b]
            own = jnp.where(b == row, 0, BLK)
            ok = (cols < upto) & (cols <= rows + own)
            bias[pl.ds(i * BLK, BLK), col(b * BLK, BLK)] = jnp.where(ok, 0.0, NEG)
        return carry

    lax.fori_loop(0, NB, fill, 0)

    chunks = (chip + 2) // 2
    plain = jnp.minimum((chip + 0) // 2, 4)

    def q_unit(p, u):
        parts = []
        for h in range(UNIT):
            part = qbuf[:, :, col(p * 1024 + (u * UNIT + h) * 128, 128)]
            parts.append(part.reshape(2 * BLK, HEAD_SIZE))
        return jnp.concatenate(parts, axis=0)

    def keys_of(buf, p, j):
        return buf[j // 2, pl.ds(lax.rem(j, 2) * 2, 2), :, col(p * 128, 128)].reshape(CH, HEAD_SIZE)

    def score(p, u, j, masked):
        slot = lax.rem(u, 2)
        sc = lax.dot_general(
            q_unit(p, u), keys_of(kbuf, p, j), (((1,), (1,)), ((), ())),
            preferred_element_type=jnp.float32,
        )
        if masked:
            add = bias[:, col(j * CH, CH)]
            sc = sc + jnp.concatenate([add] * UNIT, axis=0)
        sbuf[slot, :, col(j * CH, CH)] = sc
        top = mbuf[...]
        for t in range(CH // 128):
            top = jnp.maximum(top, sc[:, t * 128:(t + 1) * 128])
        mbuf[...] = top

    def weigh(p, u, j):
        slot = lax.rem(u, 2)
        mc = mcbuf[...]
        total = lbuf[...]
        parts = []
        for t in range(CH // 128):
            e = jnp.exp2(sbuf[slot, :, col(j * CH + t * 128, 128)] * COEF - mc)
            total = total + e
            parts.append(e.astype(jnp.bfloat16))
        lbuf[...] = total
        acc[...] += jnp.dot(
            jnp.concatenate(parts, axis=1), keys_of(vbuf, p, j), preferred_element_type=jnp.float32
        )

    def settle():
        top = jnp.max(mbuf[...], axis=1, keepdims=True) * COEF
        mcbuf[...] = jnp.broadcast_to(top, (ROWS, 128))
        mbuf[...] = jnp.full((ROWS, 128), -3e38, jnp.float32)
        lbuf[...] = jnp.zeros((ROWS, 128), jnp.float32)
        acc[...] = jnp.zeros((ROWS, HEAD_SIZE), jnp.float32)

    def loop(low, high, body):
        def step(j, carry):
            body(j)
            return carry
        lax.fori_loop(low, high, step, 0)

    def finish(p, u):
        out = acc[...] / jnp.sum(lbuf[...], axis=1, keepdims=True)
        here = lax.broadcasted_iota(jnp.int32, (BLK, HEAD_SIZE), 0)
        for i in (0, 1):
            keep = here < live_ref[0, 2 * chip + i]
            for h in range(UNIT):
                part = out[(2 * h + i) * BLK:(2 * h + i + 1) * BLK]
                obuf[i, :, col(p * 1024 + (u * UNIT + h) * 128, 128)] = jnp.where(keep, part, 0.0).astype(jnp.bfloat16)

    def send(p, u):
        for i in (0, 1):
            at_col = p * 1024 + u * (UNIT * 128)
            remote(
                obuf.at[i, :, col(at_col, UNIT * 128)],
                out_hbm.at[0, :, col(core * 4096 + at_col, UNIT * 128)],
                so.at[i], ro, across(1, i),
            ).start()

    mbuf[...] = jnp.full((ROWS, 128), -3e38, jnp.float32)
    stage2(0)
    stage1(1)
    queries(1)
    stage3(0)

    def phase(p, carry):
        @pl.when(p < 3)
        def _():
            stage2(p + 1)
        @pl.when(p < 2)
        def _():
            stage1(p + 2)
            queries(p + 2)
        arrived(p)
        loop(0, plain, lambda j: score(p, 0, j, False))
        loop(plain, chunks, lambda j: score(p, 0, j, True))
        settle()

        def unit(u, carry):
            def both(masked):
                def body(j):
                    score(p, u, j, masked)
                    weigh(p, u - 1, j)
                return body
            loop(0, plain, both(False))
            loop(plain, chunks, both(True))
            finish(p, u - 1)
            send(p, u - 1)
            settle()
            @pl.when((u == 2) & (p < 3))
            def _():
                stage3(p + 1)
            return carry

        lax.fori_loop(1, UNITS, unit, 0)
        loop(0, chunks, lambda j: weigh(p, UNITS - 1, j))
        finish(p, UNITS - 1)
        send(p, UNITS - 1)
        return carry

    lax.fori_loop(0, PHASES, phase, 0)

    wait_on(out_hbm.at[0], ro)
    for i in (0, 1):
        wait_on(obuf.at[i], so.at[i])
    wait_on(qbuf.at[0], sq)
    for n, (_, buf) in enumerate(pairs):
        for dest in range(7):
            ref = buf.at[0, pl.ds(0, 2), :, pl.ds(0, 128)]
            if dest == 0:
                wait_on(ref, s1.at[n, 0])
            else:
                wait_on(ref, s1.at[n, dest])
        for side in (0, 1):
            wait_on(buf.at[:, :, :, pl.ds(0, 128)], s2.at[n, side])
            wait_on(buf.at[pl.ds(0, 2), :, :, pl.ds(0, 128)], s3.at[n, side])


def per_device(queries, keys, values, block_mask, block_live):
    dma = pltpu.SemaphoreType.DMA
    smem = pl.BlockSpec(memory_space=pltpu.SMEM)
    hbm = pl.BlockSpec(memory_space=pl.ANY)
    return pl.pallas_call(
        kernel,
        out_shape=jax.ShapeDtypeStruct(queries.shape, queries.dtype),
        in_specs=[smem, smem, hbm, hbm, hbm],
        out_specs=hbm,
        scratch_shapes=[
            pltpu.VMEM((4, 4, 2 * BLK, 512), jnp.bfloat16),
            pltpu.VMEM((4, 4, 2 * BLK, 512), jnp.bfloat16),
            pltpu.VMEM((2, BLK, 4096), jnp.bfloat16),
            pltpu.VMEM((2, BLK, 4096), jnp.bfloat16),
            pltpu.VMEM((2, ROWS, NB * BLK), jnp.float32),
            pltpu.VMEM((2 * BLK, NB * BLK), jnp.float32),
            pltpu.VMEM((ROWS, 128), jnp.float32),
            pltpu.VMEM((ROWS, 128), jnp.float32),
            pltpu.VMEM((ROWS, 128), jnp.float32),
            pltpu.VMEM((ROWS, HEAD_SIZE), jnp.float32),
            dma((4, 2)), dma((4, 2, 2)), dma((4, 2, 2)), dma((4,)), dma,
            dma((2, 7)), dma((2, 2)), dma((2, 2)), dma, dma((2,)),
        ],
        compiler_params=pltpu.CompilerParams(
            collective_id=0, has_side_effects=True, vmem_limit_bytes=60 * 1024 * 1024
        ),
    )(block_mask, block_live, queries, keys, values)


def solution(mesh):
    placed = (
        P("section", "seq", None),
        P("section", "seq", None),
        P("section", "seq", None),
        P("section", None, None),
        P("section", None),
    )
    return jax.shard_map(
        per_device, mesh=mesh, in_specs=placed, out_specs=P("section", "seq", None), check_vma=False
    )
```

```python
import jax
import jax.numpy as jnp
from jax import lax
from jax.experimental import pallas as pl
from jax.experimental.pallas import tpu as pltpu
from jax.sharding import PartitionSpec as P

QUERY_HEADS = 64
KEY_VALUE_HEADS = 8
HEAD_SIZE = 128
BLK = 128
NB = 32
UNIT = 2
UNITS = 8 // UNIT
ROWS = 2 * BLK * UNIT
CH = 1024
STEP = 512
COEF = 1.4426950408889634 * HEAD_SIZE ** (-0.5)
NEG = -1e30


def col(start, size):
    return pl.ds(pl.multiple_of(start, 128), size)


def kernel(
    mask_ref, live_ref, q_hbm, k_hbm, v_hbm, out_hbm,
    kbuf, vbuf, kshift, vshift, qbuf, obuf, sbuf0, sbuf1, bias, reach, keep, mbuf, mcbuf, qs0, qs1, acc,
    r1, r2, r3, rq, rkv, rre, ro, s1, s2, s3, sq, sq3, skv, sre, so, so3, so4,
):
    z = lax.axis_index("section")
    s = lax.axis_index("seq")
    core = lax.rem(s, 2)
    chip = s // 2
    x = lax.rem(chip, 4)
    y = chip // 4
    last_row = y // 3

    def at(xx, yy, kk):
        return {"seq": (lax.rem(yy, 4) * 4 + lax.rem(xx, 4)) * 2 + kk}

    def across(dz, kk):
        return {"section": lax.rem(z + dz, 4), "seq": chip * 2 + kk}

    other = {"seq": chip * 2 + 1 - core}

    def remote(src, dst, send, recv, dev):
        return pltpu.make_async_remote_copy(
            src_ref=src, dst_ref=dst, send_sem=send, recv_sem=recv,
            device_id=dev, device_id_type=pl.DeviceIdType.MESH,
        )

    barrier = pltpu.get_barrier_semaphore()
    partners = [other]
    for d in (1, 2, 3):
        for kk in (0, 1):
            partners.append(at(x + d, y, kk))
            partners.append(at(x, y + d, kk))
    for d in (1, 3):
        for kk in (0, 1):
            partners.append(across(d, kk))
            partners.append({"section": lax.rem(z + d, 4), **at(x, y + d, kk)})
    for dev in partners:
        pl.semaphore_signal(barrier, inc=1, device_id=dev, device_id_type=pl.DeviceIdType.MESH)
    pl.semaphore_wait(barrier, len(partners))

    pairs = ((k_hbm, kbuf), (v_hbm, vbuf))
    shifts = (kshift, vshift)

    def stage1(p):
        for n, (src_hbm, buf) in enumerate(pairs):
            dst = buf.at[y, x, pl.ds(core * BLK, BLK), pl.ds(p * 128, 128)]
            for g in (0, 1):
                if p < 3:
                    src = src_hbm.at[0, :, pl.ds((4 * g + p) * 128, 128)]
                else:
                    src = shifts[n].at[:, pl.ds(g * 128, 128)]
                @pl.when(core == g)
                def _():
                    pltpu.make_async_copy(src, dst, r1.at[p, n]).start()
                @pl.when(core != g)
                def _():
                    remote(src, dst, s1.at[n, 0], r1.at[p, n], other).start()
                for d in (1, 3, 2):
                    dev = at(x + d, y, 0) if g == 0 else at(x, y + d, 1)
                    remote(src, dst, s1.at[n, 3 * g + d], r1.at[p, n], dev).start()

    def queries(p):
        dst = qbuf.at[p, core]
        pltpu.make_async_copy(q_hbm.at[0, :, col(core * 4096 + p * 1024, 1024)], dst, rq.at[p]).start()
        remote(q_hbm.at[0, :, col((1 - core) * 4096 + p * 1024, 1024)], dst, sq, rq.at[p], other).start()

    def shift_keys():
        for n, (src_hbm, _) in enumerate(pairs):
            for g in (0, 1):
                remote(
                    src_hbm.at[0, :, pl.ds((4 * g + 3) * 128, 128)], shifts[n].at[:, pl.ds(g * 128, 128)],
                    skv.at[n], rkv.at[n], across(1, core),
                ).start()

    def ahead(kk):
        return {"section": lax.rem(z + 1, 4), "seq": (chip - 12 * last_row) * 2 + kk}

    def shift_queries():
        for g in (0, 1):
            remote(
                q_hbm.at[0, :, pl.ds(g * 4096 + 3 * 1024, 1024)], qbuf.at[3 + last_row, core],
                sq3, rq.at[3 + last_row], ahead(g),
            ).start()

    def wait_on(ref, sem):
        pltpu.make_async_copy(ref, ref, sem).wait()

    lower, upper = (0, 1), (1, 3)
    is_first, is_second = core == 0, core == 1

    def row_in(rows):
        hit = y == rows[0]
        for r in rows[1:]:
            hit = hit | (y == r)
        return hit

    def plan(p):
        if p < 3:
            return dict(whole=((0, 1, 2), (0,)), half=((), (1,)), on=((1, 2), (0, 3)))
        return dict(whole=((0, 1, 3), (1,)), half=((2,), (0, 2)), on=((1, 3), (1, 3)))

    def moved(rows, d):
        return tuple((r + d) % 4 for r in rows)

    def second_rows(p):
        return is_second if p < 3 else is_second & (y < 3)

    def stage2(p):
        lane = pl.ds(p * 128, 128)
        for n, (_, buf) in enumerate(pairs):
            wait_on(buf.at[0, :, :, lane], r1.at[p, n])
        for n, (_, buf) in enumerate(pairs):
            for side, d in (lower, upper):
                def go(src, dev):
                    remote(src, src, s2.at[p // 3, n, side], r2.at[p, n, side], dev).start()
                for rows, part in ((plan(p)["whole"][side], pl.ds(0, 4)), (plan(p)["half"][side], pl.ds(2 * side, 2))):
                    if rows:
                        @pl.when(is_first & row_in(rows))
                        def _():
                            go(buf.at[y, part, :, lane], at(x, y + d, 0))
                @pl.when(second_rows(p))
                def _():
                    go(buf.at[:, x, :, lane], at(x + d, y, 1))

    def stage3(p):
        lane = pl.ds(p * 128, 128)
        for n, (_, buf) in enumerate(pairs):
            for side, d in (lower, upper):
                for rows, size in ((plan(p)["whole"][side], 4), (plan(p)["half"][side], 2)):
                    if rows:
                        @pl.when(is_first & row_in(moved(rows, d)))
                        def _():
                            wait_on(buf.at[0, pl.ds(0, size), :, lane], r2.at[p, n, side])
                @pl.when(second_rows(p))
                def _():
                    wait_on(buf.at[0, :, :, lane], r2.at[p, n, side])
        for n, (_, buf) in enumerate(pairs):
            for side, d in (lower, upper):
                def go(src, dev):
                    remote(src, src, s3.at[p // 3, n, side], r3.at[p, n, side], dev).start()
                @pl.when(is_first & row_in(plan(p)["on"][side]))
                def _():
                    go(buf.at[lax.rem(y + 4 - d, 4), pl.ds(2 * side, 2), :, lane], at(x, y + d, 0))
                @pl.when(second_rows(p))
                def _():
                    go(buf.at[pl.ds(2 * side, 2), lax.rem(x + 4 - d, 4), :, lane], at(x + d, y, 1))

    def arrived(p):
        for n, (_, buf) in enumerate(pairs):
            for side, d in (lower, upper):
                @pl.when((is_first & row_in(moved(plan(p)["on"][side], d))) | second_rows(p))
                def _():
                    wait_on(buf.at[0, pl.ds(0, 2), :, pl.ds(0, 128)], r3.at[p, n, side])

    stage1(0)
    queries(0)
    stage1(1)

    lanes = lax.broadcasted_iota(jnp.int32, (8, BLK), 1)
    first = lax.broadcasted_iota(jnp.int32, (8, BLK), 0) == 0

    def reach_of(b, carry):
        upto = [live_ref[0, b] * mask_ref[0, 2 * chip + i, b] for i in (0, 1)]
        reach[0, :, col((b - 16) * BLK, BLK)] = jnp.where(lanes < jnp.where(first, upto[0], upto[1]), 0.0, NEG)
        return carry

    lax.fori_loop(16, NB, reach_of, 0)
    stage2(0)
    shift_keys()
    remote(reach.at[0], reach.at[1 + last_row], sre, rre.at[last_row], ahead(core)).start()
    shift_queries()

    rows = lax.broadcasted_iota(jnp.int32, (BLK, BLK), 0)
    cols = lax.broadcasted_iota(jnp.int32, (BLK, BLK), 1)

    def fill(src, base):
        def one(b, carry):
            for i in (0, 1):
                line = reach[src, pl.ds(i, 1), col(jnp.maximum(b - 16, 0) * BLK, BLK)]
                line = jnp.where(b >= 16, line, 0.0)
                ok = cols <= rows + (base + i - b) * BLK
                bias[pl.ds(i * BLK, BLK), col(b * BLK, BLK)] = jnp.where(ok, line, NEG)
            return carry

        lax.fori_loop(0, NB, one, 0)
        for i in (0, 1):
            b = base + i
            line = reach[src, pl.ds(i, 1), col(jnp.maximum(b - 16, 0) * BLK, BLK)]
            line = jnp.where(b >= 16, line, 0.0)
            keep[i] = jnp.broadcast_to(line, (BLK, BLK)).T

    fill(0, 2 * chip)

    sbufs = (sbuf0, sbuf1)
    qbufs = (qs0, qs1)
    ones = jnp.ones((CH, 128), jnp.bfloat16)

    def split_queries(t, u):
        for h in range(UNIT):
            part = qbuf[t, :, :, pl.ds((u * UNIT + h) * 128, 128)]
            part = part.reshape(2 * BLK, HEAD_SIZE).astype(jnp.float32) * COEF
            high = part.astype(jnp.bfloat16)
            low = (part - high.astype(jnp.float32)).astype(jnp.bfloat16)
            here = pl.ds(h * 2 * BLK, 2 * BLK)
            qbufs[u % 2][here, pl.ds(0, 128)] = high
            qbufs[u % 2][here, pl.ds(128, 128)] = low

    def rows_of(buf, p, j):
        return buf[j, :, :, col(p * 128, 128)].reshape(CH, HEAD_SIZE)

    def score(p, u, j, masked):
        sbuf = sbufs[u % 2]
        k = rows_of(kbuf, p, j)
        top = mbuf[...]
        for t in range(CH // STEP):
            k_t = k[t * STEP:(t + 1) * STEP]
            sc = lax.dot_general(
                qbufs[u % 2][...], jnp.concatenate([k_t, k_t], axis=1), (((1,), (1,)), ((), ())),
                preferred_element_type=jnp.float32,
            )
            if masked:
                add = bias[:, col(j * CH + t * STEP, STEP)]
                sc = sc + jnp.concatenate([add] * UNIT, axis=0)
            sbuf[:, col(j * CH + t * STEP, STEP)] = sc
            for v in range(STEP // 128):
                top = jnp.maximum(top, sc[:, v * 128:(v + 1) * 128])
        mbuf[...] = top

    def weigh(p, u, j):
        sbuf = sbufs[u % 2]
        top = mcbuf[...]
        parts = []
        for t in range(CH // 128):
            e = jnp.exp2(sbuf[:, col(j * CH + t * 128, 128)] - top)
            parts.append(e.astype(jnp.bfloat16))
        acc[...] += jnp.dot(
            jnp.concatenate(parts, axis=1), jnp.concatenate([rows_of(vbuf, p, j), ones], axis=1),
            preferred_element_type=jnp.float32,
        )

    def settle():
        mcbuf[...] = jnp.broadcast_to(jnp.max(mbuf[...], axis=1, keepdims=True), (ROWS, 128))
        mbuf[...] = jnp.full((ROWS, 128), -3e38, jnp.float32)
        acc[...] = jnp.zeros((ROWS, 2 * HEAD_SIZE), jnp.float32)

    def loop(low, high, body):
        def step(j, carry):
            body(j)
            return carry
        lax.fori_loop(low, high, step, 0)

    def finish(t, u):
        out = acc[:, :HEAD_SIZE] / acc[:, HEAD_SIZE:]
        for i in (0, 1):
            alive = keep[i] > -1.0
            for h in range(UNIT):
                part = out[(2 * h + i) * BLK:(2 * h + i + 1) * BLK]
                obuf[t, i, :, pl.ds((u * UNIT + h) * 128, 128)] = jnp.where(alive, part, 0.0).astype(jnp.bfloat16)

    def send(t, u):
        width = UNIT * 128
        for i in (0, 1):
            src = obuf.at[t, i, :, pl.ds(u * width, width)]
            @pl.when(t < 3)
            def _():
                dst = out_hbm.at[0, :, col(core * 4096 + t * 1024 + u * width, width)]
                remote(src, dst, so.at[i], ro, across(1, i)).start()
            dst = out_hbm.at[0, :, col(core * 4096 + 3 * 1024 + u * width, width)]
            @pl.when((t == 3) & (core == i))
            def _():
                pltpu.make_async_copy(src, dst, ro).start()
            @pl.when((t == 3) & (core != i))
            def _():
                remote(src, dst, so3, ro, other).start()
            @pl.when(t == 4)
            def _():
                remote(src, dst, so4.at[i], ro, {"seq": (12 + x) * 2 + i}).start()

    mbuf[...] = jnp.full((ROWS, 128), -3e38, jnp.float32)
    stage3(0)
    stage2(1)
    stage1(2)
    queries(1)
    queries(2)
    for n in (0, 1):
        wait_on(shifts[n], rkv.at[n])
    stage1(3)

    def job(t, carry):
        p = jnp.minimum(t, 3)
        row = y + 3 * (t // 4)
        chunks = row + 1
        plain = jnp.minimum(row, 2)

        for part in range(4):
            @pl.when(t == part)
            def _():
                arrived(part)
        wait_on(qbuf.at[0], rq.at[t])
        @pl.when(t == 3)
        def _():
            wait_on(reach.at[1], rre.at[0])
            fill(1, 2 * chip)
        @pl.when(t == 4)
        def _():
            wait_on(reach.at[2], rre.at[1])
            fill(2, 2 * (12 + x))

        split_queries(t, 0)
        loop(0, plain, lambda j: score(p, 0, j, False))
        loop(plain, chunks, lambda j: score(p, 0, j, True))
        settle()

        for u in range(1, UNITS):
            split_queries(t, u)
            def both(masked):
                def body(j):
                    score(p, u, j, masked)
                    weigh(p, u - 1, j)
                return body
            loop(0, plain, both(False))
            loop(plain, chunks, both(True))
            finish(t, u - 1)
            send(t, u - 1)
            settle()
            if u == 1:
                @pl.when(t == 0)
                def _():
                    stage3(1)
                    stage2(2)
                    stage2(3)
                @pl.when(t == 1)
                def _():
                    stage3(2)
                    stage3(3)

        loop(0, chunks, lambda j: weigh(p, UNITS - 1, j))
        finish(t, UNITS - 1)
        send(t, UNITS - 1)
        return carry

    lax.fori_loop(0, 3 + (3 - y + 2) // 3 + (3 - y) // 3, job, 0)

    wait_on(out_hbm.at[0], ro)
    for i in (0, 1):
        wait_on(obuf.at[pl.ds(0, 3), i], so.at[i])
    @pl.when(y < 3)
    def _():
        wait_on(obuf.at[0, 0], so3)
    @pl.when(y == 0)
    def _():
        for i in (0, 1):
            wait_on(obuf.at[0, 0], so4.at[i])
    wait_on(qbuf.at[pl.ds(0, 3), 0], sq)
    wait_on(qbuf.at[0], sq3)
    wait_on(reach.at[0], sre)
    for n, (_, buf) in enumerate(pairs):
        wait_on(shifts[n], skv.at[n])
        for dest in range(7):
            wait_on(buf.at[0, pl.ds(0, 2), :, pl.ds(0, 128)], s1.at[n, dest])
        lane = pl.ds(0, 128)
        for g, p in ((0, 0), (1, 3)):
            times = pl.ds(0, 3) if g == 0 else pl.ds(0, 1)
            for side in (0, 1):
                for rows, size in ((plan(p)["whole"][side], 4), (plan(p)["half"][side], 2)):
                    if rows:
                        @pl.when(is_first & row_in(rows))
                        def _():
                            wait_on(buf.at[times, pl.ds(0, size), :, lane], s2.at[g, n, side])
                @pl.when(second_rows(p))
                def _():
                    wait_on(buf.at[times, pl.ds(0, 4), :, lane], s2.at[g, n, side])
                @pl.when((is_first & row_in(plan(p)["on"][side])) | second_rows(p))
                def _():
                    wait_on(buf.at[times, pl.ds(0, 2), :, lane], s3.at[g, n, side])


def per_device(queries, keys, values, block_mask, block_live):
    dma = pltpu.SemaphoreType.DMA
    smem = pl.BlockSpec(memory_space=pltpu.SMEM)
    hbm = pl.BlockSpec(memory_space=pl.ANY)
    return pl.pallas_call(
        kernel,
        out_shape=jax.ShapeDtypeStruct(queries.shape, queries.dtype),
        in_specs=[smem, smem, hbm, hbm, hbm],
        out_specs=hbm,
        scratch_shapes=[
            pltpu.VMEM((4, 4, 2 * BLK, 512), jnp.bfloat16),
            pltpu.VMEM((4, 4, 2 * BLK, 512), jnp.bfloat16),
            pltpu.VMEM((BLK, 256), jnp.bfloat16),
            pltpu.VMEM((BLK, 256), jnp.bfloat16),
            pltpu.VMEM((5, 2, BLK, 1024), jnp.bfloat16),
            pltpu.VMEM((5, 2, BLK, 1024), jnp.bfloat16),
            pltpu.VMEM((ROWS, NB * BLK), jnp.float32),
            pltpu.VMEM((ROWS, NB * BLK), jnp.float32),
            pltpu.VMEM((2 * BLK, NB * BLK), jnp.float32),
            pltpu.VMEM((3, 8, 16 * BLK), jnp.float32),
            pltpu.VMEM((2, BLK, BLK), jnp.float32),
            pltpu.VMEM((ROWS, 128), jnp.float32),
            pltpu.VMEM((ROWS, 128), jnp.float32),
            pltpu.VMEM((ROWS, 256), jnp.bfloat16),
            pltpu.VMEM((ROWS, 256), jnp.bfloat16),
            pltpu.VMEM((ROWS, 2 * HEAD_SIZE), jnp.float32),
            dma((4, 2)), dma((4, 2, 2)), dma((4, 2, 2)), dma((5,)), dma((2,)), dma((2,)), dma,
            dma((2, 7)), dma((2, 2, 2)), dma((2, 2, 2)), dma, dma, dma((2,)), dma, dma((2,)), dma, dma((2,)),
        ],
        compiler_params=pltpu.CompilerParams(
            collective_id=0, has_side_effects=True, vmem_limit_bytes=60 * 1024 * 1024
        ),
    )(block_mask, block_live, queries, keys, values)


def solution(mesh):
    placed = (
        P("section", "seq", None),
        P("section", "seq", None),
        P("section", "seq", None),
        P("section", None, None),
        P("section", None),
    )
    return jax.shard_map(
        per_device, mesh=mesh, in_specs=placed, out_specs=P("section", "seq", None), check_vma=False
    )
```

```python
import jax
import jax.numpy as jnp
from jax import lax
from jax.experimental import pallas as pl
from jax.experimental.pallas import tpu as pltpu
from jax.sharding import PartitionSpec as P

QUERY_HEADS = 64
KEY_VALUE_HEADS = 8
HEAD_SIZE = 128
BLK = 128
NB = 32
UNIT = 2
UNITS = 8 // UNIT
ROWS = 2 * BLK * UNIT
CH = 1024
STEP = 512
COEF = 1.4426950408889634 * HEAD_SIZE ** (-0.5)
NEG = -1e30


def col(start, size):
    return pl.ds(pl.multiple_of(start, 128), size)


def kernel(
    mask_ref, live_ref, q_hbm, k_hbm, v_hbm, out_hbm,
    kbuf, vbuf, kshift, vshift, qbuf, obuf, sbuf0, sbuf1, bias, reach, keep, mbuf, mcbuf, qs0, qs1, acc,
    r1, r2, r3, rq, rkv, rre, ro, s1, s2, s3, sq, sq3, sq4, skv, sre, sre2, so, so3, so4,
):
    z = lax.axis_index("section")
    s = lax.axis_index("seq")
    core = lax.rem(s, 2)
    chip = s // 2
    x = lax.rem(chip, 4)
    y = chip // 4

    def at(xx, yy, kk):
        return {"seq": (lax.rem(yy, 4) * 4 + lax.rem(xx, 4)) * 2 + kk}

    def across(dz, kk):
        return {"section": lax.rem(z + dz, 4), "seq": chip * 2 + kk}

    other = {"seq": chip * 2 + 1 - core}

    def remote(src, dst, send, recv, dev):
        return pltpu.make_async_remote_copy(
            src_ref=src, dst_ref=dst, send_sem=send, recv_sem=recv,
            device_id=dev, device_id_type=pl.DeviceIdType.MESH,
        )

    barrier = pltpu.get_barrier_semaphore()
    partners = [other]
    for d in (1, 2, 3):
        for kk in (0, 1):
            partners.append(at(x + d, y, kk))
            partners.append(at(x, y + d, kk))
    for d in (1, 3):
        for kk in (0, 1):
            partners.append(across(d, kk))
    for dev in partners:
        pl.semaphore_signal(barrier, inc=1, device_id=dev, device_id_type=pl.DeviceIdType.MESH)
    pl.semaphore_wait(barrier, len(partners))

    pairs = ((k_hbm, kbuf), (v_hbm, vbuf))
    shifts = (kshift, vshift)

    def row_in(rows):
        hit = y == rows[0]
        for r in rows[1:]:
            hit = hit | (y == r)
        return hit

    def plan(p):
        if p < 3:
            return dict(
                direct={1: (0, 1, 2), 2: (0, 1), 3: (0,)}, rows=(1, 2, 3, 4),
                whole=((0, 1, 2), (0,)), half=((), (1,)), on=((1, 2), (0, 3)),
            )
        return dict(
            direct={1: (0, 1, 3), 2: (0, 2), 3: (1,)}, rows=(4, 2, 3, 0),
            whole=((0, 1, 3), (1,)), half=((2,), (0, 2)), on=((1, 3), (1, 3)),
        )

    def split(count):
        up = min(count - 1, 1)
        return ((0, up), (up, count - up))

    def stage1(p):
        for n, (src_hbm, buf) in enumerate(pairs):
            dst = buf.at[y, x, pl.ds(core * BLK, BLK), pl.ds(p * 128, 128)]
            for g in (0, 1):
                if p < 3:
                    src = src_hbm.at[0, :, pl.ds((4 * g + p) * 128, 128)]
                else:
                    src = shifts[n].at[:, pl.ds(g * 128, 128)]
                @pl.when(core == g)
                def _():
                    pltpu.make_async_copy(src, dst, r1.at[p, n]).start()
                @pl.when(core != g)
                def _():
                    remote(src, dst, s1.at[p // 3, n, 0], r1.at[p, n], other).start()
                for d in (1, 3, 2):
                    if g == 0:
                        remote(src, dst, s1.at[p // 3, n, d], r1.at[p, n], at(x + d, y, 0)).start()
                    else:
                        @pl.when(row_in(plan(p)["direct"][d]))
                        def _():
                            remote(src, dst, s1.at[p // 3, n, 3 + d], r1.at[p, n], at(x, y + d, 1)).start()

    def queries(p):
        dst = qbuf.at[p, core]
        pltpu.make_async_copy(q_hbm.at[0, :, col(core * 4096 + p * 1024, 1024)], dst, rq.at[p]).start()
        remote(q_hbm.at[0, :, col((1 - core) * 4096 + p * 1024, 1024)], dst, sq, rq.at[p], other).start()

    def shift_keys():
        for n, (src_hbm, _) in enumerate(pairs):
            for g in (0, 1):
                remote(
                    src_hbm.at[0, :, pl.ds((4 * g + 3) * 128, 128)], shifts[n].at[:, pl.ds(g * 128, 128)],
                    skv.at[n], rkv.at[n], across(1, core),
                ).start()

    def shift_queries():
        for g in (0, 1):
            remote(
                q_hbm.at[0, :, pl.ds(g * 4096 + 3 * 1024, 1024)], qbuf.at[3, core],
                sq3, rq.at[3], across(1, g),
            ).start()

    def hand_down():
        wait_on(qbuf.at[3], rq.at[3])
        wait_on(reach.at[1], rre.at[0])
        remote(qbuf.at[3], qbuf.at[4], sq4, rq.at[4], at(x, y + 1, core)).start()
        remote(reach.at[1], reach.at[2], sre2, rre.at[1], at(x, y + 1, core)).start()

    def wait_on(ref, sem):
        pltpu.make_async_copy(ref, ref, sem).wait()

    lower, upper = (0, 1), (1, 3)
    is_first, is_second = core == 0, core == 1

    def moved(rows, d):
        return tuple((r + d) % 4 for r in rows)

    def by_count(p, body, least=0):
        for r, count in enumerate(plan(p)["rows"]):
            if max(count, least):
                @pl.when(is_second & (y == r))
                def _():
                    body(max(count, least))

    def stage2(p):
        lane = pl.ds(p * 128, 128)
        for n, (_, buf) in enumerate(pairs):
            @pl.when(is_first)
            def _():
                wait_on(buf.at[0, :, :, lane], r1.at[p, n])
            by_count(p, lambda c: wait_on(buf.at[0, pl.ds(0, c), :, lane], r1.at[p, n]), 1)
        for n, (_, buf) in enumerate(pairs):
            for side, d in (lower, upper):
                def go(src, dev):
                    remote(src, src, s2.at[p // 3, n, side], r2.at[p, n, side], dev).start()
                for rows, part in ((plan(p)["whole"][side], pl.ds(0, 4)), (plan(p)["half"][side], pl.ds(2 * side, 2))):
                    if rows:
                        @pl.when(is_first & row_in(rows))
                        def _():
                            go(buf.at[y, part, :, lane], at(x, y + d, 0))
                by_count(p, lambda c: go(buf.at[pl.ds(0, c), x, :, lane], at(x + d, y, 1)))

    def stage3(p):
        lane = pl.ds(p * 128, 128)
        for n, (_, buf) in enumerate(pairs):
            for side, d in (lower, upper):
                for rows, size in ((plan(p)["whole"][side], 4), (plan(p)["half"][side], 2)):
                    if rows:
                        @pl.when(is_first & row_in(moved(rows, d)))
                        def _():
                            wait_on(buf.at[0, pl.ds(0, size), :, lane], r2.at[p, n, side])
                by_count(p, lambda c: wait_on(buf.at[0, pl.ds(0, c), :, lane], r2.at[p, n, side]))
        for n, (_, buf) in enumerate(pairs):
            for side, d in (lower, upper):
                def go(src, dev):
                    remote(src, src, s3.at[p // 3, n, side], r3.at[p, n, side], dev).start()
                @pl.when(is_first & row_in(plan(p)["on"][side]))
                def _():
                    go(buf.at[lax.rem(y + 4 - d, 4), pl.ds(2 * side, 2), :, lane], at(x, y + d, 0))
                def pass_on(c):
                    start, size = split(c)[side]
                    if size:
                        go(buf.at[pl.ds(start, size), lax.rem(x + 4 - d, 4), :, lane], at(x + d, y, 1))
                by_count(p, pass_on)

    def arrived(p):
        for n, (_, buf) in enumerate(pairs):
            for side, d in (lower, upper):
                @pl.when(is_first & row_in(moved(plan(p)["on"][side], d)))
                def _():
                    wait_on(buf.at[0, pl.ds(0, 2), :, pl.ds(0, 128)], r3.at[p, n, side])
                def passed(c):
                    size = split(c)[side][1]
                    if size:
                        wait_on(buf.at[0, pl.ds(0, size), :, pl.ds(0, 128)], r3.at[p, n, side])
                by_count(p, passed)

    stage1(0)
    queries(0)

    lanes = lax.broadcasted_iota(jnp.int32, (8, BLK), 1)
    first = lax.broadcasted_iota(jnp.int32, (8, BLK), 0) == 0

    def reach_of(b, carry):
        upto = [live_ref[0, b] * mask_ref[0, 2 * chip + i, b] for i in (0, 1)]
        reach[0, :, col((b - 16) * BLK, BLK)] = jnp.where(lanes < jnp.where(first, upto[0], upto[1]), 0.0, NEG)
        return carry

    lax.fori_loop(16, NB, reach_of, 0)
    stage2(0)
    stage1(1)
    shift_keys()
    remote(reach.at[0], reach.at[1], sre, rre.at[0], across(1, core)).start()
    shift_queries()

    rows = lax.broadcasted_iota(jnp.int32, (BLK, BLK), 0)
    cols = lax.broadcasted_iota(jnp.int32, (BLK, BLK), 1)

    def fill(src, base):
        def one(b, carry):
            for i in (0, 1):
                line = reach[src, pl.ds(i, 1), col(jnp.maximum(b - 16, 0) * BLK, BLK)]
                line = jnp.where(b >= 16, line, 0.0)
                ok = cols <= rows + (base + i - b) * BLK
                bias[pl.ds(i * BLK, BLK), col(b * BLK, BLK)] = jnp.where(ok, line, NEG)
            return carry

        lax.fori_loop(0, NB, one, 0)
        for i in (0, 1):
            b = base + i
            line = reach[src, pl.ds(i, 1), col(jnp.maximum(b - 16, 0) * BLK, BLK)]
            line = jnp.where(b >= 16, line, 0.0)
            keep[i] = jnp.broadcast_to(line, (BLK, BLK)).T

    fill(0, 2 * chip)

    sbufs = (sbuf0, sbuf1)
    qbufs = (qs0, qs1)
    ones = jnp.ones((CH, 128), jnp.bfloat16)

    def split_queries(t, u):
        for h in range(UNIT):
            part = qbuf[t, :, :, pl.ds((u * UNIT + h) * 128, 128)]
            part = part.reshape(2 * BLK, HEAD_SIZE).astype(jnp.float32) * COEF
            high = part.astype(jnp.bfloat16)
            low = (part - high.astype(jnp.float32)).astype(jnp.bfloat16)
            here = pl.ds(h * 2 * BLK, 2 * BLK)
            qbufs[u % 2][here, pl.ds(0, 128)] = high
            qbufs[u % 2][here, pl.ds(128, 128)] = low

    def rows_of(buf, p, j):
        return buf[j, :, :, col(p * 128, 128)].reshape(CH, HEAD_SIZE)

    def score(p, u, j, masked):
        sbuf = sbufs[u % 2]
        k = rows_of(kbuf, p, j)
        top = mbuf[...]
        for t in range(CH // STEP):
            k_t = k[t * STEP:(t + 1) * STEP]
            sc = lax.dot_general(
                qbufs[u % 2][...], jnp.concatenate([k_t, k_t], axis=1), (((1,), (1,)), ((), ())),
                preferred_element_type=jnp.float32,
            )
            if masked:
                add = bias[:, col(j * CH + t * STEP, STEP)]
                sc = sc + jnp.concatenate([add] * UNIT, axis=0)
            sbuf[:, col(j * CH + t * STEP, STEP)] = sc
            for v in range(STEP // 128):
                top = jnp.maximum(top, sc[:, v * 128:(v + 1) * 128])
        mbuf[...] = top

    def weigh(p, u, j):
        sbuf = sbufs[u % 2]
        top = mcbuf[...]
        parts = []
        for t in range(CH // 128):
            e = jnp.exp2(sbuf[:, col(j * CH + t * 128, 128)] - top)
            parts.append(e.astype(jnp.bfloat16))
        acc[...] += jnp.dot(
            jnp.concatenate(parts, axis=1), jnp.concatenate([rows_of(vbuf, p, j), ones], axis=1),
            preferred_element_type=jnp.float32,
        )

    def settle():
        mcbuf[...] = jnp.broadcast_to(jnp.max(mbuf[...], axis=1, keepdims=True), (ROWS, 128))
        mbuf[...] = jnp.full((ROWS, 128), -3e38, jnp.float32)
        acc[...] = jnp.zeros((ROWS, 2 * HEAD_SIZE), jnp.float32)

    def loop(low, high, body):
        def step(j, carry):
            body(j)
            return carry
        lax.fori_loop(low, high, step, 0)

    def finish(t, u):
        out = acc[:, :HEAD_SIZE] / acc[:, HEAD_SIZE:]
        for i in (0, 1):
            alive = keep[i] > -1.0
            for h in range(UNIT):
                part = out[(2 * h + i) * BLK:(2 * h + i + 1) * BLK]
                obuf[t, i, :, pl.ds((u * UNIT + h) * 128, 128)] = jnp.where(alive, part, 0.0).astype(jnp.bfloat16)

    def send(t, u):
        width = UNIT * 128
        for i in (0, 1):
            src = obuf.at[t, i, :, pl.ds(u * width, width)]
            @pl.when(t < 3)
            def _():
                dst = out_hbm.at[0, :, col(core * 4096 + t * 1024 + u * width, width)]
                remote(src, dst, so.at[i], ro, across(1, i)).start()
            dst = out_hbm.at[0, :, col(core * 4096 + 3 * 1024 + u * width, width)]
            @pl.when((t == 3) & (core == i))
            def _():
                pltpu.make_async_copy(src, dst, ro).start()
            @pl.when((t == 3) & (core != i))
            def _():
                remote(src, dst, so3, ro, other).start()
            @pl.when(t == 4)
            def _():
                remote(src, dst, so4.at[i], ro, {"seq": (12 + x) * 2 + i}).start()

    mbuf[...] = jnp.full((ROWS, 128), -3e38, jnp.float32)
    stage3(0)
    stage2(1)
    stage1(2)
    queries(1)
    queries(2)
    for n in (0, 1):
        wait_on(shifts[n], rkv.at[n])
    stage1(3)

    def job(t, carry):
        p = jnp.minimum(t, 3)
        row = y + 3 * (t // 4)
        chunks = row + 1
        plain = jnp.minimum(row, 2)

        for part in range(4):
            @pl.when(t == part)
            def _():
                arrived(part)
        wait_on(qbuf.at[0], rq.at[t])
        @pl.when(t == 3)
        def _():
            wait_on(reach.at[1], rre.at[0])
            fill(1, 2 * chip)
        @pl.when(t == 4)
        def _():
            wait_on(reach.at[2], rre.at[1])
            fill(2, 2 * (12 + x))

        split_queries(t, 0)
        loop(0, plain, lambda j: score(p, 0, j, False))
        loop(plain, chunks, lambda j: score(p, 0, j, True))
        settle()

        for u in range(1, UNITS):
            split_queries(t, u)
            def both(masked):
                def body(j):
                    score(p, u, j, masked)
                    weigh(p, u - 1, j)
                return body
            loop(0, plain, both(False))
            loop(plain, chunks, both(True))
            finish(t, u - 1)
            send(t, u - 1)
            settle()
            if u == 1:
                @pl.when(t == 0)
                def _():
                    stage3(1)
                    stage2(2)
                    stage2(3)
                @pl.when((t == 0) & (y == 3))
                def _():
                    hand_down()
                @pl.when(t == 1)
                def _():
                    stage3(2)
                    stage3(3)

        loop(0, chunks, lambda j: weigh(p, UNITS - 1, j))
        finish(t, UNITS - 1)
        send(t, UNITS - 1)
        return carry

    lax.fori_loop(0, 3 + (3 - y + 2) // 3 + (3 - y) // 3, job, 0)

    wait_on(out_hbm.at[0], ro)
    for i in (0, 1):
        wait_on(obuf.at[pl.ds(0, 3), i], so.at[i])
    @pl.when(y < 3)
    def _():
        wait_on(obuf.at[0, 0], so3)
    @pl.when(y == 0)
    def _():
        for i in (0, 1):
            wait_on(obuf.at[0, 0], so4.at[i])
    wait_on(qbuf.at[pl.ds(0, 3), 0], sq)
    wait_on(qbuf.at[0], sq3)
    @pl.when(y == 3)
    def _():
        wait_on(qbuf.at[0], sq4)
        wait_on(reach.at[0], sre2)
    wait_on(reach.at[0], sre)
    for n, (_, buf) in enumerate(pairs):
        wait_on(shifts[n], skv.at[n])
        lane = pl.ds(0, 128)
        for g, p in ((0, 0), (1, 3)):
            times = pl.ds(0, 3) if g == 0 else pl.ds(0, 1)
            half = pl.ds(0, BLK)
            for dest in range(7):
                def sent():
                    wait_on(buf.at[times, 0, half, lane], s1.at[g, n, dest])
                if dest < 4:
                    sent()
                else:
                    pl.when(row_in(plan(p)["direct"][dest - 3]))(sent)
            for side in (0, 1):
                for rows, size in ((plan(p)["whole"][side], 4), (plan(p)["half"][side], 2)):
                    if rows:
                        @pl.when(is_first & row_in(rows))
                        def _():
                            wait_on(buf.at[times, pl.ds(0, size), :, lane], s2.at[g, n, side])
                @pl.when(is_first & row_in(plan(p)["on"][side]))
                def _():
                    wait_on(buf.at[times, pl.ds(0, 2), :, lane], s3.at[g, n, side])
                def drained(c):
                    wait_on(buf.at[times, pl.ds(0, c), :, lane], s2.at[g, n, side])
                    size = split(c)[side][1]
                    if size:
                        wait_on(buf.at[times, pl.ds(0, size), :, lane], s3.at[g, n, side])
                by_count(p, drained)


def per_device(queries, keys, values, block_mask, block_live):
    dma = pltpu.SemaphoreType.DMA
    smem = pl.BlockSpec(memory_space=pltpu.SMEM)
    hbm = pl.BlockSpec(memory_space=pl.ANY)
    return pl.pallas_call(
        kernel,
        out_shape=jax.ShapeDtypeStruct(queries.shape, queries.dtype),
        in_specs=[smem, smem, hbm, hbm, hbm],
        out_specs=hbm,
        scratch_shapes=[
            pltpu.VMEM((4, 4, 2 * BLK, 512), jnp.bfloat16),
            pltpu.VMEM((4, 4, 2 * BLK, 512), jnp.bfloat16),
            pltpu.VMEM((BLK, 256), jnp.bfloat16),
            pltpu.VMEM((BLK, 256), jnp.bfloat16),
            pltpu.VMEM((5, 2, BLK, 1024), jnp.bfloat16),
            pltpu.VMEM((5, 2, BLK, 1024), jnp.bfloat16),
            pltpu.VMEM((ROWS, NB * BLK), jnp.float32),
            pltpu.VMEM((ROWS, NB * BLK), jnp.float32),
            pltpu.VMEM((2 * BLK, NB * BLK), jnp.float32),
            pltpu.VMEM((3, 8, 16 * BLK), jnp.float32),
            pltpu.VMEM((2, BLK, BLK), jnp.float32),
            pltpu.VMEM((ROWS, 128), jnp.float32),
            pltpu.VMEM((ROWS, 128), jnp.float32),
            pltpu.VMEM((ROWS, 256), jnp.bfloat16),
            pltpu.VMEM((ROWS, 256), jnp.bfloat16),
            pltpu.VMEM((ROWS, 2 * HEAD_SIZE), jnp.float32),
            dma((4, 2)), dma((4, 2, 2)), dma((4, 2, 2)), dma((5,)), dma((2,)), dma((2,)), dma,
            dma((2, 2, 7)), dma((2, 2, 2)), dma((2, 2, 2)), dma, dma, dma, dma((2,)), dma, dma, dma((2,)), dma, dma((2,)),
        ],
        compiler_params=pltpu.CompilerParams(
            collective_id=0, has_side_effects=True, vmem_limit_bytes=60 * 1024 * 1024
        ),
    )(block_mask, block_live, queries, keys, values)


def solution(mesh):
    placed = (
        P("section", "seq", None),
        P("section", "seq", None),
        P("section", "seq", None),
        P("section", None, None),
        P("section", None),
    )
    return jax.shard_map(
        per_device, mesh=mesh, in_specs=placed, out_specs=P("section", "seq", None), check_vma=False
    )
```

```python
import jax
import jax.numpy as jnp
from jax import lax
from jax.experimental import pallas as pl
from jax.experimental.pallas import tpu as pltpu
from jax.sharding import PartitionSpec as P

QUERY_HEADS = 64
KEY_VALUE_HEADS = 8
HEAD_SIZE = 128
BLK = 128
NB = 32
UNIT = 2
UNITS = 8 // UNIT
ROWS = 2 * BLK * UNIT
CH = 1024
STEP = 1024
COEF = 1.4426950408889634 * HEAD_SIZE ** (-0.5)
NEG = -1e30


def col(start, size):
    return pl.ds(pl.multiple_of(start, 128), size)


def kernel(
    mask_ref, live_ref, q_hbm, k_hbm, v_hbm, out_hbm,
    kbuf, vbuf, kshift, vshift, qbuf, obuf, sbuf0, sbuf1, bias, reach, keep, mbuf, mcbuf, qs0, qs1, acc,
    r1, r2, r3, rq, rkv, rre, ro, s1, s2, s3, sq, sq3, sq4, skv, sre, sre2, so, so3, so4,
):
    z = lax.axis_index("section")
    s = lax.axis_index("seq")
    core = lax.rem(s, 2)
    chip = s // 2
    x = lax.rem(chip, 4)
    y = chip // 4

    def at(xx, yy, kk):
        return {"seq": (lax.rem(yy, 4) * 4 + lax.rem(xx, 4)) * 2 + kk}

    def across(dz, kk):
        return {"section": lax.rem(z + dz, 4), "seq": chip * 2 + kk}

    other = {"seq": chip * 2 + 1 - core}

    def remote(src, dst, send, recv, dev):
        return pltpu.make_async_remote_copy(
            src_ref=src, dst_ref=dst, send_sem=send, recv_sem=recv,
            device_id=dev, device_id_type=pl.DeviceIdType.MESH,
        )

    barrier = pltpu.get_barrier_semaphore()
    partners = [other]
    for d in (1, 2, 3):
        for kk in (0, 1):
            partners.append(at(x + d, y, kk))
            partners.append(at(x, y + d, kk))
    for d in (1, 3):
        for kk in (0, 1):
            partners.append(across(d, kk))
    for dev in partners:
        pl.semaphore_signal(barrier, inc=1, device_id=dev, device_id_type=pl.DeviceIdType.MESH)
    pl.semaphore_wait(barrier, len(partners))

    pairs = ((k_hbm, kbuf), (v_hbm, vbuf))
    shifts = (kshift, vshift)

    def row_in(rows):
        hit = y == rows[0]
        for r in rows[1:]:
            hit = hit | (y == r)
        return hit

    def plan(p):
        if p < 3:
            return dict(
                direct={1: (0, 1, 2), 2: (0, 1), 3: (0,)}, rows=(1, 2, 3, 4),
                whole=((0, 1, 2), (0,)), half=((), (1,)), on=((1, 2), (0, 3)),
            )
        return dict(
            direct={1: (0, 1, 3), 2: (0, 2), 3: (1,)}, rows=(4, 2, 3, 0),
            whole=((0, 1, 3), (1,)), half=((2,), (0, 2)), on=((1, 3), (1, 3)),
        )

    def split(count):
        up = min(count - 1, 1)
        return ((0, up), (up, count - up))

    def stage1(p):
        for n, (src_hbm, buf) in enumerate(pairs):
            dst = buf.at[y, x, pl.ds(core * BLK, BLK), pl.ds(p * 128, 128)]
            for g in (0, 1):
                if p < 3:
                    src = src_hbm.at[0, :, pl.ds((4 * g + p) * 128, 128)]
                else:
                    src = shifts[n].at[:, pl.ds(g * 128, 128)]
                @pl.when(core == g)
                def _():
                    pltpu.make_async_copy(src, dst, r1.at[p, n]).start()
                @pl.when(core != g)
                def _():
                    remote(src, dst, s1.at[p // 3, n, 0], r1.at[p, n], other).start()
                for d in (1, 3, 2):
                    if g == 0:
                        remote(src, dst, s1.at[p // 3, n, d], r1.at[p, n], at(x + d, y, 0)).start()
                    else:
                        @pl.when(row_in(plan(p)["direct"][d]))
                        def _():
                            remote(src, dst, s1.at[p // 3, n, 3 + d], r1.at[p, n], at(x, y + d, 1)).start()

    def queries(p):
        dst = qbuf.at[p, core]
        pltpu.make_async_copy(q_hbm.at[0, :, col(core * 4096 + p * 1024, 1024)], dst, rq.at[p]).start()
        remote(q_hbm.at[0, :, col((1 - core) * 4096 + p * 1024, 1024)], dst, sq, rq.at[p], other).start()

    def shift_keys():
        for n, (src_hbm, _) in enumerate(pairs):
            for g in (0, 1):
                remote(
                    src_hbm.at[0, :, pl.ds((4 * g + 3) * 128, 128)], shifts[n].at[:, pl.ds(g * 128, 128)],
                    skv.at[n], rkv.at[n], across(1, core),
                ).start()

    def shift_queries():
        for g in (0, 1):
            remote(
                q_hbm.at[0, :, pl.ds(g * 4096 + 3 * 1024, 1024)], qbuf.at[3, core],
                sq3, rq.at[3], across(1, g),
            ).start()

    def hand_down():
        wait_on(qbuf.at[3], rq.at[3])
        wait_on(reach.at[1], rre.at[0])
        remote(qbuf.at[3], qbuf.at[4], sq4, rq.at[4], at(x, y + 1, core)).start()
        remote(reach.at[1], reach.at[2], sre2, rre.at[1], at(x, y + 1, core)).start()

    def wait_on(ref, sem):
        pltpu.make_async_copy(ref, ref, sem).wait()

    lower, upper = (0, 1), (1, 3)
    is_first, is_second = core == 0, core == 1

    def moved(rows, d):
        return tuple((r + d) % 4 for r in rows)

    def by_count(p, body, least=0):
        for r, count in enumerate(plan(p)["rows"]):
            if max(count, least):
                @pl.when(is_second & (y == r))
                def _():
                    body(max(count, least))

    def stage2(p):
        lane = pl.ds(p * 128, 128)
        for n, (_, buf) in enumerate(pairs):
            @pl.when(is_first)
            def _():
                wait_on(buf.at[0, :, :, lane], r1.at[p, n])
            by_count(p, lambda c: wait_on(buf.at[0, pl.ds(0, c), :, lane], r1.at[p, n]), 1)
        for n, (_, buf) in enumerate(pairs):
            for side, d in (lower, upper):
                def go(src, dev):
                    remote(src, src, s2.at[p // 3, n, side], r2.at[p, n, side], dev).start()
                for rows, part in ((plan(p)["whole"][side], pl.ds(0, 4)), (plan(p)["half"][side], pl.ds(2 * side, 2))):
                    if rows:
                        @pl.when(is_first & row_in(rows))
                        def _():
                            go(buf.at[y, part, :, lane], at(x, y + d, 0))
                by_count(p, lambda c: go(buf.at[pl.ds(0, c), x, :, lane], at(x + d, y, 1)))

    def stage3(p):
        lane = pl.ds(p * 128, 128)
        for n, (_, buf) in enumerate(pairs):
            for side, d in (lower, upper):
                for rows, size in ((plan(p)["whole"][side], 4), (plan(p)["half"][side], 2)):
                    if rows:
                        @pl.when(is_first & row_in(moved(rows, d)))
                        def _():
                            wait_on(buf.at[0, pl.ds(0, size), :, lane], r2.at[p, n, side])
                by_count(p, lambda c: wait_on(buf.at[0, pl.ds(0, c), :, lane], r2.at[p, n, side]))
        for n, (_, buf) in enumerate(pairs):
            for side, d in (lower, upper):
                def go(src, dev):
                    remote(src, src, s3.at[p // 3, n, side], r3.at[p, n, side], dev).start()
                @pl.when(is_first & row_in(plan(p)["on"][side]))
                def _():
                    go(buf.at[lax.rem(y + 4 - d, 4), pl.ds(2 * side, 2), :, lane], at(x, y + d, 0))
                def pass_on(c):
                    start, size = split(c)[side]
                    if size:
                        go(buf.at[pl.ds(start, size), lax.rem(x + 4 - d, 4), :, lane], at(x + d, y, 1))
                by_count(p, pass_on)

    def arrived(p):
        for n, (_, buf) in enumerate(pairs):
            for side, d in (lower, upper):
                @pl.when(is_first & row_in(moved(plan(p)["on"][side], d)))
                def _():
                    wait_on(buf.at[0, pl.ds(0, 2), :, pl.ds(0, 128)], r3.at[p, n, side])
                def passed(c):
                    size = split(c)[side][1]
                    if size:
                        wait_on(buf.at[0, pl.ds(0, size), :, pl.ds(0, 128)], r3.at[p, n, side])
                by_count(p, passed)

    stage1(0)
    queries(0)

    lanes = lax.broadcasted_iota(jnp.int32, (8, BLK), 1)
    first = lax.broadcasted_iota(jnp.int32, (8, BLK), 0) == 0

    def reach_of(b, carry):
        upto = [live_ref[0, b] * mask_ref[0, 2 * chip + i, b] for i in (0, 1)]
        reach[0, :, col((b - 16) * BLK, BLK)] = jnp.where(lanes < jnp.where(first, upto[0], upto[1]), 0.0, NEG)
        return carry

    lax.fori_loop(16, NB, reach_of, 0)
    stage2(0)
    stage1(1)
    shift_keys()
    remote(reach.at[0], reach.at[1], sre, rre.at[0], across(1, core)).start()
    shift_queries()

    rows = lax.broadcasted_iota(jnp.int32, (BLK, BLK), 0)
    cols = lax.broadcasted_iota(jnp.int32, (BLK, BLK), 1)

    def fill(src, base):
        def one(b, carry):
            for i in (0, 1):
                line = reach[src, pl.ds(i, 1), col(jnp.maximum(b - 16, 0) * BLK, BLK)]
                line = jnp.where(b >= 16, line, 0.0)
                ok = cols <= rows + (base + i - b) * BLK
                bias[pl.ds(i * BLK, BLK), col(b * BLK, BLK)] = jnp.where(ok, line, NEG)
            return carry

        lax.fori_loop(0, NB, one, 0)
        for i in (0, 1):
            b = base + i
            line = reach[src, pl.ds(i, 1), col(jnp.maximum(b - 16, 0) * BLK, BLK)]
            line = jnp.where(b >= 16, line, 0.0)
            keep[i] = jnp.broadcast_to(line, (BLK, BLK)).T

    fill(0, 2 * chip)

    sbufs = (sbuf0, sbuf1)
    qbufs = (qs0, qs1)
    ones = jnp.ones((CH, 128), jnp.bfloat16)

    def split_queries(t, u):
        for h in range(UNIT):
            part = qbuf[t, :, :, pl.ds((u * UNIT + h) * 128, 128)]
            part = part.reshape(2 * BLK, HEAD_SIZE).astype(jnp.float32) * COEF
            high = part.astype(jnp.bfloat16)
            low = (part - high.astype(jnp.float32)).astype(jnp.bfloat16)
            here = pl.ds(h * 2 * BLK, 2 * BLK)
            qbufs[u % 2][here, pl.ds(0, 128)] = high
            qbufs[u % 2][here, pl.ds(128, 128)] = low

    def rows_of(buf, p, j):
        return buf[j, :, :, col(p * 128, 128)].reshape(CH, HEAD_SIZE)

    def score(p, u, j, masked):
        sbuf = sbufs[u % 2]
        k = rows_of(kbuf, p, j)
        top = mbuf[...]
        for t in range(CH // STEP):
            k_t = k[t * STEP:(t + 1) * STEP]
            sc = lax.dot_general(
                qbufs[u % 2][...], jnp.concatenate([k_t, k_t], axis=1), (((1,), (1,)), ((), ())),
                preferred_element_type=jnp.float32,
            )
            if masked:
                add = bias[:, col(j * CH + t * STEP, STEP)]
                sc = sc + jnp.concatenate([add] * UNIT, axis=0)
            sbuf[:, col(j * CH + t * STEP, STEP)] = sc
            for v in range(STEP // 128):
                top = jnp.maximum(top, sc[:, v * 128:(v + 1) * 128])
        mbuf[...] = top

    def weigh(p, u, j):
        sbuf = sbufs[u % 2]
        top = mcbuf[...]
        parts = []
        for t in range(CH // 128):
            e = jnp.exp2(sbuf[:, col(j * CH + t * 128, 128)] - top)
            parts.append(e.astype(jnp.bfloat16))
        acc[...] += jnp.dot(
            jnp.concatenate(parts, axis=1), jnp.concatenate([rows_of(vbuf, p, j), ones], axis=1),
            preferred_element_type=jnp.float32,
        )

    def settle():
        mcbuf[...] = jnp.broadcast_to(jnp.max(mbuf[...], axis=1, keepdims=True), (ROWS, 128))
        mbuf[...] = jnp.full((ROWS, 128), -3e38, jnp.float32)
        acc[...] = jnp.zeros((ROWS, 2 * HEAD_SIZE), jnp.float32)

    def loop(low, high, body):
        def step(j, carry):
            body(j)
            return carry
        lax.fori_loop(low, high, step, 0)

    def finish(t, u):
        out = acc[:, :HEAD_SIZE] / acc[:, HEAD_SIZE:]
        for i in (0, 1):
            alive = keep[i] > -1.0
            for h in range(UNIT):
                part = out[(2 * h + i) * BLK:(2 * h + i + 1) * BLK]
                obuf[t, i, :, pl.ds((u * UNIT + h) * 128, 128)] = jnp.where(alive, part, 0.0).astype(jnp.bfloat16)

    def send(t, u):
        width = UNIT * 128
        for i in (0, 1):
            src = obuf.at[t, i, :, pl.ds(u * width, width)]
            @pl.when(t < 3)
            def _():
                dst = out_hbm.at[0, :, col(core * 4096 + t * 1024 + u * width, width)]
                remote(src, dst, so.at[i], ro, across(1, i)).start()
            dst = out_hbm.at[0, :, col(core * 4096 + 3 * 1024 + u * width, width)]
            @pl.when((t == 3) & (core == i))
            def _():
                pltpu.make_async_copy(src, dst, ro).start()
            @pl.when((t == 3) & (core != i))
            def _():
                remote(src, dst, so3, ro, other).start()
            @pl.when(t == 4)
            def _():
                remote(src, dst, so4.at[i], ro, {"seq": (12 + x) * 2 + i}).start()

    mbuf[...] = jnp.full((ROWS, 128), -3e38, jnp.float32)
    stage3(0)
    stage2(1)
    stage1(2)
    queries(1)
    queries(2)
    for n in (0, 1):
        wait_on(shifts[n], rkv.at[n])
    stage1(3)

    def job(t, carry):
        p = jnp.minimum(t, 3)
        row = y + 3 * (t // 4)
        chunks = row + 1
        plain = jnp.minimum(row, 2)

        for part in range(4):
            @pl.when(t == part)
            def _():
                arrived(part)
        wait_on(qbuf.at[0], rq.at[t])
        @pl.when(t == 3)
        def _():
            wait_on(reach.at[1], rre.at[0])
            fill(1, 2 * chip)
        @pl.when(t == 4)
        def _():
            wait_on(reach.at[2], rre.at[1])
            fill(2, 2 * (12 + x))

        split_queries(t, 0)
        loop(0, plain, lambda j: score(p, 0, j, False))
        loop(plain, chunks, lambda j: score(p, 0, j, True))
        settle()
        @pl.when(t == 1)
        def _():
            stage3(2)

        for u in range(1, UNITS):
            split_queries(t, u)
            def both(masked):
                def body(j):
                    score(p, u, j, masked)
                    weigh(p, u - 1, j)
                return body
            loop(0, plain, both(False))
            loop(plain, chunks, both(True))
            finish(t, u - 1)
            send(t, u - 1)
            settle()
            if u == 1:
                @pl.when(t == 0)
                def _():
                    stage3(1)
                    stage2(2)
                    stage2(3)
                @pl.when((t == 0) & (y == 3))
                def _():
                    hand_down()
                @pl.when(t == 1)
                def _():
                    stage3(3)

        loop(0, chunks, lambda j: weigh(p, UNITS - 1, j))
        finish(t, UNITS - 1)
        send(t, UNITS - 1)
        return carry

    lax.fori_loop(0, 3 + (3 - y + 2) // 3 + (3 - y) // 3, job, 0)

    wait_on(out_hbm.at[0], ro)
    for i in (0, 1):
        wait_on(obuf.at[pl.ds(0, 3), i], so.at[i])
    @pl.when(y < 3)
    def _():
        wait_on(obuf.at[0, 0], so3)
    @pl.when(y == 0)
    def _():
        for i in (0, 1):
            wait_on(obuf.at[0, 0], so4.at[i])
    wait_on(qbuf.at[pl.ds(0, 3), 0], sq)
    wait_on(qbuf.at[0], sq3)
    @pl.when(y == 3)
    def _():
        wait_on(qbuf.at[0], sq4)
        wait_on(reach.at[0], sre2)
    wait_on(reach.at[0], sre)
    for n, (_, buf) in enumerate(pairs):
        wait_on(shifts[n], skv.at[n])
        lane = pl.ds(0, 128)
        for g, p in ((0, 0), (1, 3)):
            times = pl.ds(0, 3) if g == 0 else pl.ds(0, 1)
            half = pl.ds(0, BLK)
            for dest in range(7):
                def sent():
                    wait_on(buf.at[times, 0, half, lane], s1.at[g, n, dest])
                if dest < 4:
                    sent()
                else:
                    pl.when(row_in(plan(p)["direct"][dest - 3]))(sent)
            for side in (0, 1):
                for rows, size in ((plan(p)["whole"][side], 4), (plan(p)["half"][side], 2)):
                    if rows:
                        @pl.when(is_first & row_in(rows))
                        def _():
                            wait_on(buf.at[times, pl.ds(0, size), :, lane], s2.at[g, n, side])
                @pl.when(is_first & row_in(plan(p)["on"][side]))
                def _():
                    wait_on(buf.at[times, pl.ds(0, 2), :, lane], s3.at[g, n, side])
                def drained(c):
                    wait_on(buf.at[times, pl.ds(0, c), :, lane], s2.at[g, n, side])
                    size = split(c)[side][1]
                    if size:
                        wait_on(buf.at[times, pl.ds(0, size), :, lane], s3.at[g, n, side])
                by_count(p, drained)


def per_device(queries, keys, values, block_mask, block_live):
    dma = pltpu.SemaphoreType.DMA
    smem = pl.BlockSpec(memory_space=pltpu.SMEM)
    hbm = pl.BlockSpec(memory_space=pl.ANY)
    return pl.pallas_call(
        kernel,
        out_shape=jax.ShapeDtypeStruct(queries.shape, queries.dtype),
        in_specs=[smem, smem, hbm, hbm, hbm],
        out_specs=hbm,
        scratch_shapes=[
            pltpu.VMEM((4, 4, 2 * BLK, 512), jnp.bfloat16),
            pltpu.VMEM((4, 4, 2 * BLK, 512), jnp.bfloat16),
            pltpu.VMEM((BLK, 256), jnp.bfloat16),
            pltpu.VMEM((BLK, 256), jnp.bfloat16),
            pltpu.VMEM((5, 2, BLK, 1024), jnp.bfloat16),
            pltpu.VMEM((5, 2, BLK, 1024), jnp.bfloat16),
            pltpu.VMEM((ROWS, NB * BLK), jnp.float32),
            pltpu.VMEM((ROWS, NB * BLK), jnp.float32),
            pltpu.VMEM((2 * BLK, NB * BLK), jnp.float32),
            pltpu.VMEM((3, 8, 16 * BLK), jnp.float32),
            pltpu.VMEM((2, BLK, BLK), jnp.float32),
            pltpu.VMEM((ROWS, 128), jnp.float32),
            pltpu.VMEM((ROWS, 128), jnp.float32),
            pltpu.VMEM((ROWS, 256), jnp.bfloat16),
            pltpu.VMEM((ROWS, 256), jnp.bfloat16),
            pltpu.VMEM((ROWS, 2 * HEAD_SIZE), jnp.float32),
            dma((4, 2)), dma((4, 2, 2)), dma((4, 2, 2)), dma((5,)), dma((2,)), dma((2,)), dma,
            dma((2, 2, 7)), dma((2, 2, 2)), dma((2, 2, 2)), dma, dma, dma, dma((2,)), dma, dma, dma((2,)), dma, dma((2,)),
        ],
        compiler_params=pltpu.CompilerParams(
            collective_id=0, has_side_effects=True, vmem_limit_bytes=60 * 1024 * 1024
        ),
    )(block_mask, block_live, queries, keys, values)


def solution(mesh):
    placed = (
        P("section", "seq", None),
        P("section", "seq", None),
        P("section", "seq", None),
        P("section", None, None),
        P("section", None),
    )
    return jax.shard_map(
        per_device, mesh=mesh, in_specs=placed, out_specs=P("section", "seq", None), check_vma=False
    )
```
